32 devices in a mesh: ty: 4 (over y, x), tx: 8 (over z, core).
Axes of the slice: x: 2, y: 2, z: 4, core: 2. Of those that a mesh axis runs over, the one named last changes fastest.
Arguments:
- state: float32 [3, 512, 4096], P(None, 'ty', 'tx'), may hold values from -6 to 6
- cut_mask: int32 [512, 4096], P('ty', 'tx'), may hold values from 0 to 1, as said below
- fraction: int32 [512, 4096], P('ty', 'tx'), may hold values from 256 to 1024
- neighbourhood: int32 [512, 4096], P('ty', 'tx'), may hold values from 16 to 511, as said below
- tile_flags: int32 [4, 32], P('ty', 'tx'), may hold values from 0 to 1, as said below
- centroid_offset: float32 [2, 512, 4096], P(None, 'ty', 'tx'), may hold values from -0.45 to 0.45
Outputs:
- redistributed: float32 [3, 512, 4096], P(None, 'ty', 'tx')
The draws below stay inside these ranges and needn't reach their ends.
Inputs may be any that keep to these rules, and one draw needn't show every extreme that they name: Bit 3 (dy + 1) + (dx + 1) says whether the cell dy rows and dx columns away belongs to the cell's neighbourhood; bit 4 is always set, and no bit names a cell outside the grid. At the four corner cells of every block of 128 x 512 cells (rows k * 128 and k * 128 + 127, likewise for columns) every bit that names a cell inside the grid is set. `tile_flags`: the tiles at the four corners of every block of 128 x 512 cells are flagged. `cut_mask`: the four corner cells of every block of 128 x 512 cells are cut.
All inputs are finite; a program needn't handle non-finite values.
Results may differ from the reference program's by a relative error of at most 0.0003.
Values sent between devices are 32-bit elements; how exact they have to be, the bound alone decides.
A program may use at most 64 MiB of HBM per device.

```python
import jax
import jax.numpy as jnp
from jax import lax

ROWS = 128
COLS = 512
TILE = 128
STEPS = 1
GRID_ROWS = 512
GRID_COLS = 4096


def block_corners(shape_cells, block_rows, block_cols):
    row_index = lax.broadcasted_iota(jnp.int32, shape_cells, 0) % block_rows
    col_index = lax.broadcasted_iota(jnp.int32, shape_cells, 1) % block_cols
    row_edge = (row_index == 0) | (row_index == block_rows - 1)
    col_edge = (col_index == 0) | (col_index == block_cols - 1)
    return row_edge & col_edge


def draw_cut_mask(key, part):
    shape_cells = (GRID_ROWS, GRID_COLS)
    random_bits = jax.random.randint(key, shape_cells, 0, 2, dtype=jnp.int32)
    corner = block_corners(shape_cells, ROWS, COLS)
    return jnp.where(corner, 1, random_bits).astype(jnp.int32)


def draw_neighbourhood(key, part):
    shape_cells = (GRID_ROWS, GRID_COLS)
    random_bits = jax.random.randint(key, shape_cells, 0, 512, dtype=jnp.int32)
    corner = block_corners(shape_cells, ROWS, COLS)
    random_bits = jnp.where(corner, 511, random_bits).astype(jnp.int32)
    row_index = lax.broadcasted_iota(jnp.int32, shape_cells, 0)
    col_index = lax.broadcasted_iota(jnp.int32, shape_cells, 1)
    allowed = jnp.zeros(shape_cells, jnp.int32)
    bit_index = 0
    for row_step in (-1, 0, 1):
        for col_step in (-1, 0, 1):
            inside = (row_index + row_step >= 0) & (row_index + row_step < GRID_ROWS)
            inside = inside & (col_index + col_step >= 0) & (col_index + col_step < GRID_COLS)
            allowed = allowed + jnp.where(inside, 1 << bit_index, 0).astype(jnp.int32)
            bit_index = bit_index + 1
    return (random_bits | 16) & allowed


def draw_tile_flags(key, part):
    shape_tiles = (GRID_ROWS // TILE, GRID_COLS // TILE)
    scores = jax.random.randint(key, shape_tiles, 0, 1024, dtype=jnp.int32)
    col_index = lax.broadcasted_iota(jnp.int32, shape_tiles, 1)
    span_tiles = max(shape_tiles[1] - 1, 1)
    threshold = 120 + 880 * col_index // span_tiles
    corner = block_corners(shape_tiles, ROWS // TILE, COLS // TILE)
    return jnp.where(corner, 1, (scores < threshold).astype(jnp.int32)).astype(jnp.int32)


def with_ends(values, stream_key, low, high):
    longest = values.shape.index(max(values.shape))
    spots = []
    for shift in (0, 1):
        where = [jax.random.randint(jax.random.fold_in(stream_key, axis), (), 0, length) for axis, length in enumerate(values.shape)]
        where[longest] = (where[longest] + shift) % values.shape[longest]
        spots.append(tuple(where))
    return values.at[spots[0]].set(low).at[spots[1]].set(high)


def level_of(rng, extent, cuts, low, largest):
    loudness, own = 1.0, jax.random.fold_in(rng, 6)
    for dim, parts in cuts:
        draws = jnp.exp(jax.random.uniform(jax.random.fold_in(own, dim), (parts,), jnp.float32, low / len(cuts), largest / len(cuts)))
        loudness = loudness * jnp.repeat(draws, extent[dim] // parts).reshape([-1 if axis == dim else 1 for axis in range(len(extent))])
    return loudness


def gaussian(rng, dims, scale, most, shards=(), held_as=jnp.bfloat16):
    gain = level_of(rng, dims, shards, -0.22, 0.18) if shards else 1.0
    values = jax.random.normal(rng, dims, jnp.float32) * scale * gain
    return jnp.minimum(jnp.maximum(values, -most), most).astype(held_as)


def setup_inputs(seed: int = 0) -> dict:
    keys = jax.random.split(jax.random.key(seed), 7)
    return {
        "state": gaussian(keys[0], (3, GRID_ROWS, GRID_COLS), 1.0, 6.0, ((1, 4), (2, 8)), jnp.float32),
        "cut_mask": draw_cut_mask(jax.random.fold_in(keys[6], 71), 0),
        "fraction": with_ends(jax.random.randint(keys[2], (GRID_ROWS, GRID_COLS), 256, 1025), jax.random.fold_in(keys[2], 1), 256, 1024).astype(jnp.int32),
        "neighbourhood": draw_neighbourhood(jax.random.fold_in(keys[6], 71), 0),
        "tile_flags": draw_tile_flags(jax.random.fold_in(keys[6], 71), 0),
        "centroid_offset": jnp.clip(jax.random.uniform(keys[5], (2, GRID_ROWS, GRID_COLS), jnp.float32, -0.45, 0.45) * level_of(keys[5], (2, GRID_ROWS, GRID_COLS), ((1, 4), (2, 8)), -0.4, 0.0), -0.45, 0.45),
    }


courant = 0.1
cell_offsets = [(row_step, col_step) for row_step in (-1, 0, 1) for col_step in (-1, 0, 1)]


def window(padded, row_step, col_step):
    height = padded.shape[-2] - 2
    width = padded.shape[-1] - 2
    return padded[..., 1 + row_step:1 + row_step + height, 1 + col_step:1 + col_step + width]


def spread(values, row_step, col_step):
    widths = [(0, 0)] * (values.ndim - 2) + [(1 + row_step, 1 - row_step), (1 + col_step, 1 - col_step)]
    return jnp.pad(values, widths)


def pad_cells(values):
    widths = [(0, 0)] * (values.ndim - 2) + [(1, 1), (1, 1)]
    return jnp.pad(values, widths)


def members_of(code_bits, active):
    result = []
    for bit_index in range(9):
        bit_value = jnp.right_shift(code_bits, bit_index) & 1
        centre_value = 1 if bit_index == 4 else 0
        result.append(jnp.where(active > 0, bit_value, centre_value).astype(jnp.float32))
    return result


def advance(padded, inv_volume):
    centre = window(padded, 0, 0)
    eastern = window(padded, 0, 1)
    western = window(padded, 0, -1)
    northern = window(padded, 1, 0)
    southern = window(padded, -1, 0)
    mass_flux = 0.5 * ((eastern[1] - western[1]) + (northern[2] - southern[2]))
    xmom_flux = 0.5 * (eastern[0] - western[0])
    ymom_flux = 0.5 * (northern[0] - southern[0])
    smoothing = eastern + western + northern + southern - 4.0 * centre
    divergence = jnp.stack([mass_flux, xmom_flux, ymom_flux]) - 0.5 * smoothing
    return centre - courant * inv_volume * divergence


def geometry(members, share_pad, offset_pad):
    total = 0.0
    sum_x = 0.0
    sum_y = 0.0
    for bit_index, (row_step, col_step) in enumerate(cell_offsets):
        weight = members[bit_index] * window(share_pad, row_step, col_step)
        total = total + weight
        sum_x = sum_x + weight * (col_step + window(offset_pad[0], row_step, col_step))
        sum_y = sum_y + weight * (row_step + window(offset_pad[1], row_step, col_step))
    return total, jnp.stack([sum_x / total, sum_y / total])


def averages(members, share_pad, star_pad, total):
    summed = 0.0
    for bit_index, (row_step, col_step) in enumerate(cell_offsets):
        weight = members[bit_index] * window(share_pad, row_step, col_step)
        summed = summed + weight * window(star_pad, row_step, col_step)
    return summed / total


def slopes(average, average_pad, centroid, centroid_pad):
    moment_xx = 1.0
    moment_xy = 0.0
    moment_yy = 1.0
    right_x = 0.0
    right_y = 0.0
    for row_step, col_step in cell_offsets:
        if row_step == 0 and col_step == 0:
            continue
        apart_x = col_step + window(centroid_pad[0], row_step, col_step) - centroid[0]
        apart_y = row_step + window(centroid_pad[1], row_step, col_step) - centroid[1]
        change = window(average_pad, row_step, col_step) - average
        moment_xx = moment_xx + apart_x * apart_x
        moment_xy = moment_xy + apart_x * apart_y
        moment_yy = moment_yy + apart_y * apart_y
        right_x = right_x + apart_x * change
        right_y = right_y + apart_y * change
    determinant = moment_xx * moment_yy - moment_xy * moment_xy
    slope_x = (moment_yy * right_x - moment_xy * right_y) / determinant
    slope_y = (moment_xx * right_y - moment_xy * right_x) / determinant
    return slope_x, slope_y


def pushed(members, kappa_cell, average, slope_x, slope_y, centroid, offset_pad):
    extended = 0.0
    for bit_index, (row_step, col_step) in enumerate(cell_offsets):
        toward_x = col_step + window(offset_pad[0], row_step, col_step) - centroid[0]
        toward_y = row_step + window(offset_pad[1], row_step, col_step) - centroid[1]
        value = (members[bit_index] * kappa_cell) * (average + slope_x * toward_x + slope_y * toward_y)
        extended = extended + spread(value, row_step, col_step)
    return extended


def reference(state, cut_mask, fraction, neighbourhood, tile_flags, centroid_offset):
    flag_cells = jnp.repeat(jnp.repeat(tile_flags, TILE, axis=0), TILE, axis=1)
    active = flag_cells * cut_mask
    kappa_cell = jnp.where(active > 0, fraction.astype(jnp.float32) * (1.0 / 1024.0), 1.0).astype(jnp.float32)
    inv_volume = 1.0 / kappa_cell
    offset_cell = centroid_offset * active.astype(jnp.float32)
    members = members_of(neighbourhood, active)
    gathered = 0.0
    for bit_index, (row_step, col_step) in enumerate(cell_offsets):
        gathered = gathered + spread(members[bit_index] * kappa_cell, row_step, col_step)
    coverage = gathered[1:-1, 1:-1]
    share_cell = kappa_cell / coverage
    share_pad = pad_cells(share_cell)
    offset_pad = pad_cells(offset_cell)
    total, centroid = geometry(members, share_pad, offset_pad)
    centroid_pad = pad_cells(centroid)

    def one_step(step_index, current):
        star = advance(pad_cells(current), inv_volume)
        average = averages(members, share_pad, pad_cells(star), total)
        slope_x, slope_y = slopes(average, pad_cells(average), centroid, centroid_pad)
        extended = pushed(members, kappa_cell, average, slope_x, slope_y, centroid, offset_pad)
        return extended[:, 1:-1, 1:-1] / coverage

    return lax.fori_loop(0, STEPS, one_step, state)
```

```python
import functools

import jax
import jax.numpy as jnp
from jax import lax
from jax.experimental import pallas as pl
from jax.experimental.pallas import tpu as pltpu
from jax.sharding import PartitionSpec as P

COURANT = 0.1
LANES = 128
SUBS = 8
DEPTH = 4
TINY = 1.0 / 1024.0
STEPS = (-1, 0, 1)
DIRS = [(dy, dx) for dy in STEPS for dx in STEPS if (dy, dx) != (0, 0)]
UNROLL = True


def bit_of(dy, dx):
    return 1 << (3 * (dy + 1) + dx + 1)


def lanes_from(value, step):
    return value if step == 0 else pltpu.roll(value, (-step) % LANES, 1)


def kernel(
    state, active, fraction, code, offset, out,
    fbuf, ibuf, obuf, ce, kp, st, of, ic, gf, af, pf,
    lsem, ssem, rsem,
):
    ny, nx = lax.axis_size("ty"), lax.axis_size("tx")
    y, x = lax.axis_index("ty"), lax.axis_index("tx")
    height = state.shape[1]
    tiles = state.shape[2] // LANES
    strip = (height + 2 * DEPTH) // SUBS
    inner = pl.ds(SUBS, height)

    local = []
    for t in range(tiles):
        cols = pl.ds(t * LANES, LANES)
        pairs = [
            (active.at[:, cols], ibuf.at[0, t + 1, inner]),
            (fraction.at[:, cols], ibuf.at[1, t + 1, inner]),
            (code.at[:, cols], ibuf.at[2, t + 1, inner]),
            (state.at[:, :, cols], fbuf.at[pl.ds(0, 3), t + 1, inner]),
            (offset.at[:, :, cols], fbuf.at[pl.ds(3, 2), t + 1, inner]),
        ]
        for src, dst in pairs:
            copy = pltpu.make_async_copy(src, dst, lsem.at[len(local)])
            copy.start()
            local.append(copy)

    def exists(dy, dx):
        good = None
        for step, place, size in ((dy, y, ny), (dx, x, nx)):
            if step:
                here = place > 0 if step < 0 else place < size - 1
                good = here if good is None else good & here
        return good

    barrier = pltpu.get_barrier_semaphore()
    for dy, dx in DIRS:
        @pl.when(exists(dy, dx))
        def _(dy=dy, dx=dx):
            pl.semaphore_signal(
                barrier, inc=1, device_id=(y + dy, x + dx),
                device_id_type=pl.DeviceIdType.MESH,
            )

    rows_of = {-1: pl.ds(0, SUBS), 0: inner, 1: pl.ds(SUBS + height, SUBS)}
    cols_of = {-1: pl.ds(0, 1), 0: pl.ds(1, tiles), 1: pl.ds(tiles + 1, 1)}
    for dy, dx in DIRS:
        @pl.when(jnp.logical_not(exists(dy, dx)))
        def _(dy=dy, dx=dx):
            part = (cols_of[dx], rows_of[dy])
            shape = (cols_of[dx].size, rows_of[dy].size, LANES)
            for k in range(5):
                fbuf[(k,) + part] = jnp.zeros(shape, jnp.float32)
            for k in range(3):
                ibuf[(k,) + part] = jnp.full(shape, 1 if k == 0 else 0, jnp.int32)

    for copy in local:
        copy.wait()
    has = lambda good: jnp.where(good, 1, 0).astype(jnp.int32)
    pl.semaphore_wait(barrier, sum(has(exists(dy, dx)) for dy, dx in DIRS))

    def message(k, g):
        dy, dx = DIRS[k]
        buf = (ibuf, fbuf)[g]
        src_rows = {-1: pl.ds(SUBS, SUBS), 0: inner, 1: pl.ds(height, SUBS)}[dy]
        src_cols = {-1: pl.ds(1, 1), 0: pl.ds(1, tiles), 1: pl.ds(tiles, 1)}[dx]
        return pltpu.make_async_remote_copy(
            src_ref=buf.at[:, src_cols, src_rows],
            dst_ref=buf.at[:, cols_of[-dx], rows_of[-dy]],
            send_sem=ssem.at[2 * k + g],
            recv_sem=rsem.at[2 * k + g],
            device_id=(y + dy, x + dx),
            device_id_type=pl.DeviceIdType.MESH,
        )

    vertical = [k for k, d in enumerate(DIRS) if d[1] == 0]
    sideways = [k for k, d in enumerate(DIRS) if d[1] != 0]
    corners = [k for k in sideways if DIRS[k][0] != 0]
    level = [k for k in sideways if DIRS[k][0] == 0]
    for group, ks in ((0, vertical), (1, vertical), (0, level), (1, level), (0, corners), (1, corners)):
        for k in ks:
            @pl.when(exists(*DIRS[k]))
            def _(k=k, group=group):
                message(k, group).start()

    def await_all(ks, group):
        for k in ks:
            dy, dx = DIRS[k]
            @pl.when(exists(-dy, -dx))
            def _(k=k):
                message(k, group).wait_recv()

    await_all(vertical, 0)
    await_all(vertical, 1)

    step = (state.shape[2] - (LANES - 2 * DEPTH)) // tiles
    lane = lax.broadcasted_iota(jnp.int32, (SUBS, LANES), 1)

    def each_row(fn):
        if UNROLL is True:
            for r in range(strip):
                fn(r)
        else:
            def one(r, carry):
                fn(r)
                return carry
            lax.fori_loop(0, strip, one, 0, unroll=UNROLL)

    def wrap(ref, *index):
        ref[(*index, 0)] = pltpu.roll(ref[(*index, strip)], 1, 0)
        ref[(*index, strip + 1)] = pltpu.roll(ref[(*index, 1)], SUBS - 1, 0)

    def tile_work(c):
        turn = DEPTH + c * (LANES - step)
        first = lane >= LANES - turn

        def pick(buf, k, r):
            rows = pl.ds(DEPTH + r, SUBS, stride=strip)
            both = jnp.where(first, buf[k, c, rows, :], buf[k, c + 1, rows, :])
            return pltpu.roll(both, turn, 1)

        def load_row(r):
            on = pick(ibuf, 0, r) > 0
            ce[r + 1] = jnp.where(on, pick(ibuf, 2, r), 16)
            kp[r + 1] = jnp.where(on, pick(ibuf, 1, r).astype(jnp.float32) * (1.0 / 1024.0), 1.0)
            for k in range(3):
                st[k, r + 1] = pick(fbuf, k, r)
            for k in range(2):
                of[k, r + 1] = jnp.where(on, pick(fbuf, 3 + k, r), 0.0)

        each_row(load_row)
        wrap(ce)
        wrap(kp)
        for k in range(3):
            wrap(st, k)

        def share_row(r):
            sums = {}
            for dx in STEPS:
                parts = [
                    jnp.where((ce[r + 1 - dy] & bit_of(dy, dx)) != 0, kp[r + 1 - dy], 0.0)
                    for dy in STEPS
                ]
                sums[dx] = parts[0] + parts[1] + parts[2]
            cover = sums[0] + lanes_from(sums[1], -1) + lanes_from(sums[-1], 1)
            inv_cover = 1.0 / jnp.maximum(cover, TINY)
            ic[r] = inv_cover
            kappa = kp[r + 1]
            share = kappa * inv_cover
            rate = COURANT / jnp.maximum(kappa, TINY)
            here = [st[k, r + 1] for k in range(3)]
            east = [lanes_from(v, 1) for v in here]
            west = [lanes_from(v, -1) for v in here]
            north = [st[k, r + 2] for k in range(3)]
            south = [st[k, r] for k in range(3)]
            flux = [
                (east[1] - west[1]) + (north[2] - south[2]),
                east[0] - west[0],
                north[0] - south[0],
            ]
            gf[0, r + 1] = share
            gf[1, r + 1] = share * of[0, r + 1]
            gf[2, r + 1] = share * of[1, r + 1]
            for k in range(3):
                smooth = (east[k] + west[k]) + (north[k] + south[k]) - 4.0 * here[k]
                gf[3 + k, r + 1] = share * (here[k] - (0.5 * rate) * (flux[k] - smooth))

        each_row(share_row)
        for k in range(6):
            wrap(gf, k)

        def gather_row(r):
            own = ce[r + 1]
            rows = {dy: [gf[k, r + 1 + dy] for k in range(6)] for dy in STEPS}
            for dy in (-1, 1):
                rows[dy][2] = rows[dy][2] + dy * rows[dy][0]
            sums = {}
            for dx in STEPS:
                moved = lanes_from(own, -dx)
                total = [None] * 6
                for dy in STEPS:
                    member = (moved & bit_of(dy, dx)) != 0
                    for k in range(6):
                        term = jnp.where(member, rows[dy][k], 0.0)
                        total[k] = term if total[k] is None else total[k] + term
                sums[dx] = [lanes_from(v, dx) for v in total]
            whole = [sums[0][k] + sums[1][k] + sums[-1][k] for k in range(6)]
            inv_total = 1.0 / jnp.maximum(whole[0], TINY)
            cx = (whole[1] + (sums[1][0] - sums[-1][0])) * inv_total
            cy = whole[2] * inv_total
            avg = [whole[3 + k] * inv_total for k in range(3)]
            values = [cx, cy, cx * cx, cx * cy, cy * cy]
            values += avg + [cx * a for a in avg] + [cy * a for a in avg]
            for k, v in enumerate(values):
                af[k, r + 1] = v

        each_row(gather_row)
        for k in range(14):
            wrap(af, k)

        def slope_row(r):
            def column(k):
                return af[k, r] + af[k, r + 1] + af[k, r + 2]

            def rise(k):
                return af[k, r + 2] - af[k, r]

            def box(v):
                return v + lanes_from(v, 1) + lanes_from(v, -1)

            def tilted(v, slant):
                return v + lanes_from(v + slant, 1) + lanes_from(v - slant, -1)

            cx, cy = af[0, r + 1], af[1, r + 1]
            col_cx, col_cy = column(0), column(1)
            sum_x, sum_y = box(col_cx), box(col_cy)
            far_x, far_y = sum_x - 9.0 * cx, sum_y - 9.0 * cy
            m_xx = 7.0 + tilted(column(2), 2.0 * col_cx) - cx * (sum_x + far_x)
            m_yy = 7.0 + box(column(4) + 2.0 * rise(1)) - cy * (sum_y + far_y)
            m_xy = tilted(column(3) + rise(0), col_cy) - cx * sum_y - cy * far_x
            inv_det = 1.0 / (m_xx * m_yy - m_xy * m_xy)
            kappa_det = kp[r + 1] * inv_det
            i_xx, i_yy, i_xy = m_yy * kappa_det, m_xx * kappa_det, m_xy * kappa_det
            for k in range(3):
                a = af[5 + k, r + 1]
                col_a = column(5 + k)
                sum_a = box(col_a)
                v_x = tilted(column(8 + k), col_a) - cx * sum_a - a * far_x
                v_y = box(column(11 + k) + rise(5 + k)) - cy * sum_a - a * far_y
                s_x = i_xx * v_x - i_xy * v_y
                s_y = i_yy * v_y - i_xy * v_x
                pf[k, r + 1] = kp[r + 1] * a - s_x * cx - s_y * cy
                pf[3 + k, r + 1] = s_x
                pf[6 + k, r + 1] = s_y

        each_row(slope_row)
        for k in range(9):
            wrap(pf, k)

        back = LANES - turn

        def push_row(r):
            sums = {}
            off_x, off_y = of[0, r + 1], of[1, r + 1]
            for dx in STEPS:
                to_x = lanes_from(off_x, dx) + dx
                to_y = lanes_from(off_y, dx)
                total = [None] * 3
                for dy in STEPS:
                    i = r + 1 - dy
                    member = (ce[i] & bit_of(dy, dx)) != 0
                    up = to_y + dy if dy else to_y
                    for k in range(3):
                        value = pf[k, i] + pf[3 + k, i] * to_x + pf[6 + k, i] * up
                        term = jnp.where(member, value, 0.0)
                        total[k] = term if total[k] is None else total[k] + term
                sums[dx] = [lanes_from(v, -dx) for v in total]
            for k in range(3):
                value = (sums[0][k] + sums[1][k] + sums[-1][k]) * ic[r]
                obuf[k, c, pl.ds(DEPTH + r, SUBS, stride=strip), :] = pltpu.roll(value, back, 1)

        each_row(push_row)

    def tile_step(k, carry):
        c = jnp.where(k < tiles - 1, k + 1, jnp.where(k == tiles - 1, 0, tiles))

        @pl.when(k == tiles - 1)
        def _():
            await_all(sideways, 0)
            await_all(sideways, 1)

        tile_work(c)
        return carry

    lax.fori_loop(0, tiles + 1, tile_step, 0)

    for t in range(tiles):
        edge = (t + 1) * step - t * LANES + (LANES - 2 * DEPTH - step) // 2
        for r in range(height // SUBS):
            rows = pl.ds(SUBS * (r + 1), SUBS)
            for k in range(3):
                out[k, pl.ds(SUBS * r, SUBS), pl.ds(t * LANES, LANES)] = jnp.where(
                    lane < edge, obuf[k, t, rows, :], obuf[k, t + 1, rows, :]
                )

    for k in range(len(DIRS)):
        @pl.when(exists(*DIRS[k]))
        def _(k=k):
            for group in (0, 1):
                message(k, group).wait_send()


def body(state, cut_mask, fraction, neighbourhood, tile_flags, centroid_offset):
    height, width = cut_mask.shape
    flag_rows, flag_cols = tile_flags.shape
    tile_h, tile_w = height // flag_rows, width // flag_cols
    flag_cells = jnp.broadcast_to(
        tile_flags[:, None, :, None], (flag_rows, tile_h, flag_cols, tile_w)
    ).reshape(height, width)
    active = flag_cells * cut_mask
    tiles = width // LANES
    strip = (height + 2 * DEPTH) // SUBS
    step = (width - (LANES - 2 * DEPTH)) // tiles
    assert strip * SUBS == height + 2 * DEPTH and tiles * LANES == width
    assert step * tiles + LANES - 2 * DEPTH == width and height % SUBS == 0
    tall = (tiles + 2, height + 2 * SUBS, LANES)
    rows = (strip + 2, SUBS, LANES)
    f32, i32 = jnp.float32, jnp.int32
    return pl.pallas_call(
        kernel,
        out_shape=jax.ShapeDtypeStruct(state.shape, state.dtype),
        in_specs=[pl.BlockSpec(memory_space=pl.ANY)] * 5,
        out_specs=pl.BlockSpec(memory_space=pltpu.VMEM),
        scratch_shapes=[
            pltpu.VMEM((5,) + tall, f32),
            pltpu.VMEM((3,) + tall, i32),
            pltpu.VMEM((3, tiles + 1) + tall[1:], f32),
            pltpu.VMEM(rows, i32),
            pltpu.VMEM(rows, f32),
            pltpu.VMEM((3,) + rows, f32),
            pltpu.VMEM((2,) + rows, f32),
            pltpu.VMEM(rows, f32),
            pltpu.VMEM((6,) + rows, f32),
            pltpu.VMEM((14,) + rows, f32),
            pltpu.VMEM((9,) + rows, f32),
            pltpu.SemaphoreType.DMA((5 * tiles,)),
            pltpu.SemaphoreType.DMA((2 * len(DIRS),)),
            pltpu.SemaphoreType.DMA((2 * len(DIRS),)),
        ],
        compiler_params=pltpu.CompilerParams(collective_id=0, has_side_effects=True),
    )(state, active, fraction, neighbourhood, centroid_offset)


def solution(mesh):
    placed = (
        P(None, "ty", "tx"),
        P("ty", "tx"),
        P("ty", "tx"),
        P("ty", "tx"),
        P("ty", "tx"),
        P(None, "ty", "tx"),
    )
    return jax.shard_map(
        body, mesh=mesh, in_specs=placed, out_specs=P(None, "ty", "tx"), check_vma=False
    )
```

```python
import functools

import jax
import jax.numpy as jnp
from jax import lax
from jax.experimental import pallas as pl
from jax.experimental.pallas import tpu as pltpu
from jax.sharding import PartitionSpec as P

COURANT = 0.1
LANES = 128
SUBS = 8
DEPTH = 4
TINY = 1.0 / 1024.0
STEPS = (-1, 0, 1)
DIRS = [(dy, dx) for dy in STEPS for dx in STEPS if (dy, dx) != (0, 0)]
GROUP = 8


def index_of(dy, dx):
    return 3 * (dy + 1) + dx + 1


def bit_of(dy, dx):
    return 1 << index_of(dy, dx)


def lanes_from(value, step):
    return value if step == 0 else pltpu.roll(value, (-step) % LANES, 1)


def kernel(
    state, active, fraction, code, offset, out,
    fbuf, ibuf, obuf, ce, kp, kb, st, of, ic, gf, af, hf, pf,
    lsem, ssem, rsem,
):
    ny, nx = lax.axis_size("ty"), lax.axis_size("tx")
    y, x = lax.axis_index("ty"), lax.axis_index("tx")
    height = state.shape[1]
    tiles = state.shape[2] // LANES
    strip = (height + 2 * DEPTH) // SUBS
    inner = pl.ds(SUBS, height)

    local = []
    for t in range(tiles):
        cols = pl.ds(t * LANES, LANES)
        pairs = [
            (active.at[:, cols], ibuf.at[0, t + 1, inner]),
            (fraction.at[:, cols], ibuf.at[1, t + 1, inner]),
            (code.at[:, cols], ibuf.at[2, t + 1, inner]),
            (state.at[:, :, cols], fbuf.at[pl.ds(0, 3), t + 1, inner]),
            (offset.at[:, :, cols], fbuf.at[pl.ds(3, 2), t + 1, inner]),
        ]
        for src, dst in pairs:
            copy = pltpu.make_async_copy(src, dst, lsem.at[len(local)])
            copy.start()
            local.append(copy)

    def exists(dy, dx):
        good = None
        for step, place, size in ((dy, y, ny), (dx, x, nx)):
            if step:
                here = place > 0 if step < 0 else place < size - 1
                good = here if good is None else good & here
        return good

    barrier = pltpu.get_barrier_semaphore()
    for dy, dx in DIRS:
        @pl.when(exists(dy, dx))
        def _(dy=dy, dx=dx):
            pl.semaphore_signal(
                barrier, inc=1, device_id=(y + dy, x + dx),
                device_id_type=pl.DeviceIdType.MESH,
            )

    rows_of = {-1: pl.ds(0, SUBS), 0: inner, 1: pl.ds(SUBS + height, SUBS)}
    cols_of = {-1: pl.ds(0, 1), 0: pl.ds(1, tiles), 1: pl.ds(tiles + 1, 1)}
    for dy, dx in DIRS:
        @pl.when(jnp.logical_not(exists(dy, dx)))
        def _(dy=dy, dx=dx):
            part = (cols_of[dx], rows_of[dy])
            shape = (cols_of[dx].size, rows_of[dy].size, LANES)
            for k in range(5):
                fbuf[(k,) + part] = jnp.zeros(shape, jnp.float32)
            for k in range(3):
                ibuf[(k,) + part] = jnp.full(shape, 1 if k == 0 else 0, jnp.int32)

    for copy in local:
        copy.wait()
    has = lambda good: jnp.where(good, 1, 0).astype(jnp.int32)
    pl.semaphore_wait(barrier, sum(has(exists(dy, dx)) for dy, dx in DIRS))

    def message(k, g):
        dy, dx = DIRS[k]
        buf = (ibuf, fbuf)[g]
        src_rows = {-1: pl.ds(SUBS, SUBS), 0: inner, 1: pl.ds(height, SUBS)}[dy]
        src_cols = {-1: pl.ds(1, 1), 0: pl.ds(1, tiles), 1: pl.ds(tiles, 1)}[dx]
        return pltpu.make_async_remote_copy(
            src_ref=buf.at[:, src_cols, src_rows],
            dst_ref=buf.at[:, cols_of[-dx], rows_of[-dy]],
            send_sem=ssem.at[2 * k + g],
            recv_sem=rsem.at[2 * k + g],
            device_id=(y + dy, x + dx),
            device_id_type=pl.DeviceIdType.MESH,
        )

    vertical = [k for k, d in enumerate(DIRS) if d[1] == 0]
    sideways = [k for k, d in enumerate(DIRS) if d[1] != 0]
    corners = [k for k in sideways if DIRS[k][0] != 0]
    level = [k for k in sideways if DIRS[k][0] == 0]
    for group, ks in ((0, vertical), (1, vertical), (0, level), (1, level), (0, corners), (1, corners)):
        for k in ks:
            @pl.when(exists(*DIRS[k]))
            def _(k=k, group=group):
                message(k, group).start()

    def await_all(ks, group):
        for k in ks:
            dy, dx = DIRS[k]
            @pl.when(exists(-dy, -dx))
            def _(k=k):
                message(k, group).wait_recv()

    await_all(vertical, 0)
    await_all(vertical, 1)

    step = (state.shape[2] - (LANES - 2 * DEPTH)) // tiles
    lane = lax.broadcasted_iota(jnp.int32, (SUBS, LANES), 1)

    def each_row(fn):
        groups = strip // GROUP if GROUP < strip else 0

        def some(g, carry):
            for r in range(GROUP):
                fn(g * GROUP + r)
            return carry

        if groups:
            lax.fori_loop(0, groups, some, 0)
        for r in range(groups * GROUP, strip):
            fn(r)

    def wrap(ref, *index):
        ref[(*index, 0)] = pltpu.roll(ref[(*index, strip)], 1, 0)
        ref[(*index, strip + 1)] = pltpu.roll(ref[(*index, 1)], SUBS - 1, 0)

    def tile_work(c):
        turn = DEPTH + c * (LANES - step)
        first = lane >= LANES - turn

        def load_row(r):
            rows = pl.ds(DEPTH + r, SUBS, stride=strip)

            def pick(buf, k):
                return jnp.where(first, buf[k, c, rows, :], buf[k, c + 1, rows, :])

            def turned(value):
                return pltpu.roll(value, turn, 1)

            on = pick(ibuf, 0) > 0
            bits = turned(jnp.where(on, pick(ibuf, 2), 16))
            kappa = turned(
                jnp.where(on, pick(ibuf, 1).astype(jnp.float32) * (1.0 / 1024.0), 1.0)
            )
            ce[r] = bits
            kp[r] = kappa
            for b in range(9):
                kb[b, r + 1] = jnp.where((bits & (1 << b)) != 0, kappa, 0.0)
            for k in range(3):
                st[k, r + 1] = turned(pick(fbuf, k))
            for k in range(2):
                of[k, r] = turned(jnp.where(on, pick(fbuf, 3 + k), 0.0))

        each_row(load_row)
        for k in range(9):
            wrap(kb, k)
        for k in range(3):
            wrap(st, k)

        def share_row(r):
            sums = {}
            for dx in STEPS:
                parts = [kb[index_of(dy, dx), r + 1 - dy] for dy in STEPS]
                sums[dx] = parts[0] + parts[1] + parts[2]
            cover = sums[0] + lanes_from(sums[1], -1) + lanes_from(sums[-1], 1)
            inv_cover = 1.0 / jnp.maximum(cover, TINY)
            ic[r] = inv_cover
            kappa = kp[r]
            share = kappa * inv_cover
            rate = (0.5 * COURANT) / jnp.maximum(kappa, TINY)
            here = [st[k, r + 1] for k in range(3)]
            east = [lanes_from(v, 1) for v in here]
            west = [lanes_from(v, -1) for v in here]
            north = [st[k, r + 2] for k in range(3)]
            south = [st[k, r] for k in range(3)]
            flux = [
                (east[1] - west[1]) + (north[2] - south[2]),
                east[0] - west[0],
                north[0] - south[0],
            ]
            gf[0, r + 1] = share
            gf[1, r + 1] = share * of[0, r]
            gf[2, r + 1] = share * of[1, r]
            for k in range(3):
                smooth = (east[k] + west[k]) + (north[k] + south[k]) - 4.0 * here[k]
                gf[3 + k, r + 1] = share * (here[k] - rate * (flux[k] - smooth))

        each_row(share_row)
        for k in range(6):
            wrap(gf, k)

        def gather_row(r):
            own = ce[r]
            rows = {dy: [gf[k, r + 1 + dy] for k in range(6)] for dy in STEPS}
            for dy in (-1, 1):
                rows[dy][2] = rows[dy][2] + dy * rows[dy][0]
            sums = {}
            for dx in STEPS:
                moved = lanes_from(own, -dx)
                total = [None] * 6
                for dy in STEPS:
                    member = (moved & bit_of(dy, dx)) != 0
                    for k in range(6):
                        term = jnp.where(member, rows[dy][k], 0.0)
                        total[k] = term if total[k] is None else total[k] + term
                sums[dx] = [lanes_from(v, dx) for v in total]
            whole = [sums[0][k] + sums[1][k] + sums[-1][k] for k in range(6)]
            inv_total = 1.0 / jnp.maximum(whole[0], TINY)
            cx = (whole[1] + (sums[1][0] - sums[-1][0])) * inv_total
            cy = whole[2] * inv_total
            av = [whole[3 + k] * inv_total for k in range(3)]
            ux = [lanes_from(cx, -1) - 1.0, cx, lanes_from(cx, 1) + 1.0]
            uy = [lanes_from(cy, dx) for dx in STEPS]

            def dot(left, right):
                return left[0] * right[0] + left[1] * right[1] + left[2] * right[2]

            values = [ux[0] + ux[1] + ux[2], uy[0] + uy[1] + uy[2]]
            values += [dot(ux, ux), dot(ux, uy), dot(uy, uy)]
            for k in range(3):
                near = [lanes_from(av[k], dx) for dx in STEPS]
                values += [near[0] + near[1] + near[2], dot(ux, near), dot(uy, near)]
            for k, v in enumerate(values):
                hf[k, r + 1] = v
            for k, v in enumerate([cx, cy] + av):
                af[k, r] = v

        each_row(gather_row)
        for k in range(14):
            wrap(hf, k)

        def slope_row(r):
            def column(k):
                low, high = hf[k, r], hf[k, r + 2]
                return low + hf[k, r + 1] + high, high - low

            def total(k):
                return hf[k, r] + hf[k, r + 1] + hf[k, r + 2]

            cx, cy = af[0, r], af[1, r]
            sum_x, rise_x = column(0)
            sum_y, rise_y = column(1)
            far_x, far_y = sum_x - 9.0 * cx, sum_y - 9.0 * cy
            m_xx = total(2) + 1.0 - cx * (sum_x + far_x)
            m_xy = total(3) + rise_x - cx * sum_y - cy * far_x
            m_yy = total(4) + 7.0 + 2.0 * rise_y - cy * (sum_y + far_y)
            scale = 1.0 / (m_xx * m_yy - m_xy * m_xy)
            i_xx, i_yy, i_xy = m_yy * scale, m_xx * scale, m_xy * scale
            for k in range(3):
                a = af[2 + k, r]
                sum_a, rise_a = column(5 + 3 * k)
                v_x = total(6 + 3 * k) - cx * sum_a - a * far_x
                v_y = total(7 + 3 * k) + rise_a - cy * sum_a - a * far_y
                s_x = i_xx * v_x - i_xy * v_y
                s_y = i_yy * v_y - i_xy * v_x
                pf[k, r + 1] = a - s_x * cx - s_y * cy
                pf[3 + k, r + 1] = s_x
                pf[6 + k, r + 1] = s_y

        each_row(slope_row)
        for k in range(9):
            wrap(pf, k)

        back = LANES - turn

        def push_row(r):
            sums = {}
            off_x, off_y = of[0, r], of[1, r]
            for dx in STEPS:
                to_x = lanes_from(off_x, dx)
                to_x = to_x + dx if dx else to_x
                to_y = lanes_from(off_y, dx)
                total = [None] * 3
                for dy in STEPS:
                    i = r + 1 - dy
                    weight = kb[index_of(dy, dx), i]
                    up = to_y + dy if dy else to_y
                    for k in range(3):
                        value = pf[k, i] + pf[3 + k, i] * to_x + pf[6 + k, i] * up
                        term = weight * value
                        total[k] = term if total[k] is None else total[k] + term
                sums[dx] = [lanes_from(v, -dx) for v in total]
            for k in range(3):
                value = (sums[0][k] + sums[1][k] + sums[-1][k]) * ic[r]
                obuf[k, c, pl.ds(DEPTH + r, SUBS, stride=strip), :] = pltpu.roll(value, back, 1)

        each_row(push_row)

    def tile_step(k, carry):
        c = jnp.where(k < tiles - 1, k + 1, jnp.where(k == tiles - 1, 0, tiles))

        @pl.when(k == tiles - 1)
        def _():
            await_all(sideways, 0)
            await_all(sideways, 1)

        tile_work(c)
        return carry

    lax.fori_loop(0, tiles + 1, tile_step, 0)

    for t in range(tiles):
        edge = (t + 1) * step - t * LANES + (LANES - 2 * DEPTH - step) // 2
        for r in range(height // SUBS):
            rows = pl.ds(SUBS * (r + 1), SUBS)
            for k in range(3):
                out[k, pl.ds(SUBS * r, SUBS), pl.ds(t * LANES, LANES)] = jnp.where(
                    lane < edge, obuf[k, t, rows, :], obuf[k, t + 1, rows, :]
                )

    for k in range(len(DIRS)):
        @pl.when(exists(*DIRS[k]))
        def _(k=k):
            for group in (0, 1):
                message(k, group).wait_send()


def body(state, cut_mask, fraction, neighbourhood, tile_flags, centroid_offset):
    height, width = cut_mask.shape
    flag_rows, flag_cols = tile_flags.shape
    tile_h, tile_w = height // flag_rows, width // flag_cols
    flag_cells = jnp.broadcast_to(
        tile_flags[:, None, :, None], (flag_rows, tile_h, flag_cols, tile_w)
    ).reshape(height, width)
    active = flag_cells * cut_mask
    tiles = width // LANES
    strip = (height + 2 * DEPTH) // SUBS
    step = (width - (LANES - 2 * DEPTH)) // tiles
    assert strip * SUBS == height + 2 * DEPTH and tiles * LANES == width
    assert step * tiles + LANES - 2 * DEPTH == width and height % SUBS == 0
    tall = (tiles + 2, height + 2 * SUBS, LANES)
    rows = (strip + 2, SUBS, LANES)
    flat = (strip, SUBS, LANES)
    f32, i32 = jnp.float32, jnp.int32
    return pl.pallas_call(
        kernel,
        out_shape=jax.ShapeDtypeStruct(state.shape, state.dtype),
        in_specs=[pl.BlockSpec(memory_space=pl.ANY)] * 5,
        out_specs=pl.BlockSpec(memory_space=pltpu.VMEM),
        scratch_shapes=[
            pltpu.VMEM((5,) + tall, f32),
            pltpu.VMEM((3,) + tall, i32),
            pltpu.VMEM((3, tiles + 1) + tall[1:], f32),
            pltpu.VMEM(flat, i32),
            pltpu.VMEM(flat, f32),
            pltpu.VMEM((9,) + rows, f32),
            pltpu.VMEM((3,) + rows, f32),
            pltpu.VMEM((2,) + flat, f32),
            pltpu.VMEM(flat, f32),
            pltpu.VMEM((6,) + rows, f32),
            pltpu.VMEM((5,) + flat, f32),
            pltpu.VMEM((14,) + rows, f32),
            pltpu.VMEM((9,) + rows, f32),
            pltpu.SemaphoreType.DMA((5 * tiles,)),
            pltpu.SemaphoreType.DMA((2 * len(DIRS),)),
            pltpu.SemaphoreType.DMA((2 * len(DIRS),)),
        ],
        compiler_params=pltpu.CompilerParams(collective_id=0, has_side_effects=True),
    )(state, active, fraction, neighbourhood, centroid_offset)


def solution(mesh):
    placed = (
        P(None, "ty", "tx"),
        P("ty", "tx"),
        P("ty", "tx"),
        P("ty", "tx"),
        P("ty", "tx"),
        P(None, "ty", "tx"),
    )
    return jax.shard_map(
        body, mesh=mesh, in_specs=placed, out_specs=P(None, "ty", "tx"), check_vma=False
    )
```

```python
import functools

import jax
import jax.numpy as jnp
from jax import lax
from jax.experimental import pallas as pl
from jax.experimental.pallas import tpu as pltpu
from jax.sharding import PartitionSpec as P

COURANT = 0.1
LANES = 128
SUBS = 8
DEPTH = 4
TINY = 1.0 / 1024.0
STEPS = (-1, 0, 1)
DIRS = [(dy, dx) for dy in STEPS for dx in STEPS if (dy, dx) != (0, 0)]
GROUP = 8


def index_of(dy, dx):
    return 3 * (dy + 1) + dx + 1


def bit_of(dy, dx):
    return 1 << index_of(dy, dx)


def lanes_from(value, step):
    return value if step == 0 else pltpu.roll(value, (-step) % LANES, 1)


def kernel(
    state, mask, fraction, code, flags, offset, out,
    fbuf, ibuf, fl, ft, fr, obuf, ce, kp, kb, st, of, ic, gf, af, hf, pf,
    lsem, ssem, rsem,
):
    ny, nx = lax.axis_size("ty"), lax.axis_size("tx")
    y, x = lax.axis_index("ty"), lax.axis_index("tx")
    height = state.shape[1]
    tiles = state.shape[2] // LANES
    strip = (height + 2 * DEPTH) // SUBS
    inner = pl.ds(SUBS, height)

    local = []
    for t in range(tiles):
        cols = pl.ds(t * LANES, LANES)
        pairs = [
            (mask.at[:, cols], ibuf.at[0, t + 1, inner]),
            (fraction.at[:, cols], ibuf.at[1, t + 1, inner]),
            (code.at[:, cols], ibuf.at[2, t + 1, inner]),
            (state.at[:, :, cols], fbuf.at[pl.ds(0, 3), t + 1, inner]),
            (offset.at[:, :, cols], fbuf.at[pl.ds(3, 2), t + 1, inner]),
        ]
        for src, dst in pairs:
            copy = pltpu.make_async_copy(src, dst, lsem.at[len(local)])
            copy.start()
            local.append(copy)

    copy = pltpu.make_async_copy(flags, fl.at[1, 1], lsem.at[len(local)])
    copy.start()
    local.append(copy)

    def exists(dy, dx):
        good = None
        for step, place, size in ((dy, y, ny), (dx, x, nx)):
            if step:
                here = place > 0 if step < 0 else place < size - 1
                good = here if good is None else good & here
        return good

    barrier = pltpu.get_barrier_semaphore()
    for dy, dx in DIRS:
        @pl.when(exists(dy, dx))
        def _(dy=dy, dx=dx):
            pl.semaphore_signal(
                barrier, inc=1, device_id=(y + dy, x + dx),
                device_id_type=pl.DeviceIdType.MESH,
            )

    rows_of = {-1: pl.ds(DEPTH, DEPTH), 0: inner, 1: pl.ds(SUBS + height, DEPTH)}
    cols_of = {-1: pl.ds(0, 1), 0: pl.ds(1, tiles), 1: pl.ds(tiles + 1, 1)}
    for dy, dx in DIRS:
        @pl.when(jnp.logical_not(exists(dy, dx)))
        def _(dy=dy, dx=dx):
            part = (cols_of[dx], rows_of[dy])
            shape = (cols_of[dx].size, rows_of[dy].size, LANES)
            fl[dy + 1, dx + 1] = jnp.ones((1, tiles), jnp.int32)
            for k in range(5):
                fbuf[(k,) + part] = jnp.zeros(shape, jnp.float32)
            for k in range(3):
                ibuf[(k,) + part] = jnp.full(shape, 1 if k == 0 else 0, jnp.int32)

    for copy in local:
        copy.wait()
    has = lambda good: jnp.where(good, 1, 0).astype(jnp.int32)
    pl.semaphore_wait(barrier, sum(has(exists(dy, dx)) for dy, dx in DIRS))

    def message(k, g):
        dy, dx = DIRS[k]
        where = dict(
            send_sem=ssem.at[3 * k + g],
            recv_sem=rsem.at[3 * k + g],
            device_id=(y + dy, x + dx),
            device_id_type=pl.DeviceIdType.MESH,
        )
        if g == 2:
            return pltpu.make_async_remote_copy(
                src_ref=fl.at[1, 1], dst_ref=fl.at[1 - dy, 1 - dx], **where
            )
        buf = (ibuf, fbuf)[g]
        src_rows = {-1: pl.ds(SUBS, DEPTH), 0: inner, 1: pl.ds(height + DEPTH, DEPTH)}[dy]
        src_cols = {-1: pl.ds(1, 1), 0: pl.ds(1, tiles), 1: pl.ds(tiles, 1)}[dx]
        return pltpu.make_async_remote_copy(
            src_ref=buf.at[:, src_cols, src_rows],
            dst_ref=buf.at[:, cols_of[-dx], rows_of[-dy]],
            **where,
        )

    vertical = [k for k, d in enumerate(DIRS) if d[1] == 0]
    sideways = [k for k, d in enumerate(DIRS) if d[1] != 0]
    corners = [k for k in sideways if DIRS[k][0] != 0]
    level = [k for k in sideways if DIRS[k][0] == 0]
    order = ((2, vertical), (0, vertical), (1, vertical), (2, corners), (0, corners), (1, corners))
    order += ((2, level), (0, level), (1, level))
    for group, ks in order:
        for k in ks:
            @pl.when(exists(*DIRS[k]))
            def _(k=k, group=group):
                message(k, group).start()

    def await_all(ks, group):
        for k in ks:
            dy, dx = DIRS[k]
            @pl.when(exists(-dy, -dx))
            def _(k=k):
                message(k, group).wait_recv()

    def spread_flags(side, tile, place):
        for g in range(3):
            value = fl[g, side, :, pl.ds(tile, 1)]
            ft[g, place] = jnp.broadcast_to(value, (SUBS, LANES))

    for group in (2, 0, 1):
        await_all(vertical, group)
    for t in range(tiles):
        spread_flags(1, t, t + 1)

    step = (state.shape[2] - (LANES - 2 * DEPTH)) // tiles
    lane = lax.broadcasted_iota(jnp.int32, (SUBS, LANES), 1)
    sub = lax.broadcasted_iota(jnp.int32, (SUBS, LANES), 0)

    def each_row(fn):
        groups = strip // GROUP if GROUP < strip else 0

        def some(g, carry):
            for r in range(GROUP):
                fn(g * GROUP + r)
            return carry

        if groups:
            lax.fori_loop(0, groups, some, 0)
        for r in range(groups * GROUP, strip):
            fn(r)

    def wrap(ref, *index):
        ref[(*index, 0)] = pltpu.roll(ref[(*index, strip)], 1, 0)
        ref[(*index, strip + 1)] = pltpu.roll(ref[(*index, 1)], SUBS - 1, 0)

    def tile_work(c):
        turn = DEPTH + c * (LANES - step)
        first = lane >= LANES - turn

        flag = [jnp.where(first, ft[g, c], ft[g, c + 1]) for g in range(3)]
        for r in range(strip):
            value = flag[1]
            if r < DEPTH:
                value = jnp.where(sub == 0, flag[0], value)
            if r >= strip - DEPTH:
                value = jnp.where(sub == SUBS - 1, flag[2], value)
            fr[r] = value

        def load_row(r):
            rows = pl.ds(DEPTH + r, SUBS, stride=strip)

            def pick(buf, k):
                return jnp.where(first, buf[k, c, rows, :], buf[k, c + 1, rows, :])

            def turned(value):
                return pltpu.roll(value, turn, 1)

            on = pick(ibuf, 0) * fr[r] > 0
            bits = turned(jnp.where(on, pick(ibuf, 2), 16))
            kappa = turned(
                jnp.where(on, pick(ibuf, 1).astype(jnp.float32) * (1.0 / 1024.0), 1.0)
            )
            ce[r] = bits
            kp[r] = kappa
            for b in range(9):
                kb[b, r + 1] = jnp.where((bits & (1 << b)) != 0, kappa, 0.0)
            for k in range(3):
                st[k, r + 1] = turned(pick(fbuf, k))
            for k in range(2):
                of[k, r] = turned(jnp.where(on, pick(fbuf, 3 + k), 0.0))

        each_row(load_row)
        for k in range(9):
            wrap(kb, k)
        for k in range(3):
            wrap(st, k)

        def share_row(r):
            sums = {}
            for dx in STEPS:
                parts = [kb[index_of(dy, dx), r + 1 - dy] for dy in STEPS]
                sums[dx] = parts[0] + parts[1] + parts[2]
            cover = sums[0] + lanes_from(sums[1], -1) + lanes_from(sums[-1], 1)
            inv_cover = 1.0 / jnp.maximum(cover, TINY)
            ic[r] = inv_cover
            kappa = kp[r]
            share = kappa * inv_cover
            rate = (0.5 * COURANT) / jnp.maximum(kappa, TINY)
            here = [st[k, r + 1] for k in range(3)]
            east = [lanes_from(v, 1) for v in here]
            west = [lanes_from(v, -1) for v in here]
            north = [st[k, r + 2] for k in range(3)]
            south = [st[k, r] for k in range(3)]
            flux = [
                (east[1] - west[1]) + (north[2] - south[2]),
                east[0] - west[0],
                north[0] - south[0],
            ]
            gf[0, r + 1] = share
            gf[1, r + 1] = share * of[0, r]
            gf[2, r + 1] = share * of[1, r]
            for k in range(3):
                smooth = (east[k] + west[k]) + (north[k] + south[k]) - 4.0 * here[k]
                gf[3 + k, r + 1] = share * (here[k] - rate * (flux[k] - smooth))

        each_row(share_row)
        for k in range(6):
            wrap(gf, k)

        def gather_row(r):
            own = ce[r]
            rows = {dy: [gf[k, r + 1 + dy] for k in range(6)] for dy in STEPS}
            for dy in (-1, 1):
                rows[dy][2] = rows[dy][2] + dy * rows[dy][0]
            sums = {}
            for dx in STEPS:
                moved = lanes_from(own, -dx)
                total = [None] * 6
                for dy in STEPS:
                    member = (moved & bit_of(dy, dx)) != 0
                    for k in range(6):
                        term = jnp.where(member, rows[dy][k], 0.0)
                        total[k] = term if total[k] is None else total[k] + term
                sums[dx] = [lanes_from(v, dx) for v in total]
            whole = [sums[0][k] + sums[1][k] + sums[-1][k] for k in range(6)]
            inv_total = 1.0 / jnp.maximum(whole[0], TINY)
            cx = (whole[1] + (sums[1][0] - sums[-1][0])) * inv_total
            cy = whole[2] * inv_total
            av = [whole[3 + k] * inv_total for k in range(3)]
            ux = [lanes_from(cx, -1) - 1.0, cx, lanes_from(cx, 1) + 1.0]
            uy = [lanes_from(cy, dx) for dx in STEPS]

            def dot(left, right):
                return left[0] * right[0] + left[1] * right[1] + left[2] * right[2]

            values = [ux[0] + ux[1] + ux[2], uy[0] + uy[1] + uy[2]]
            values += [dot(ux, ux), dot(ux, uy), dot(uy, uy)]
            for k in range(3):
                near = [lanes_from(av[k], dx) for dx in STEPS]
                values += [near[0] + near[1] + near[2], dot(ux, near), dot(uy, near)]
            for k, v in enumerate(values):
                hf[k, r + 1] = v
            for k, v in enumerate([cx, cy] + av):
                af[k, r] = v

        each_row(gather_row)
        for k in range(14):
            wrap(hf, k)

        def slope_row(r):
            def column(k):
                low, high = hf[k, r], hf[k, r + 2]
                return low + hf[k, r + 1] + high, high - low

            def total(k):
                return hf[k, r] + hf[k, r + 1] + hf[k, r + 2]

            cx, cy = af[0, r], af[1, r]
            sum_x, rise_x = column(0)
            sum_y, rise_y = column(1)
            far_x, far_y = sum_x - 9.0 * cx, sum_y - 9.0 * cy
            m_xx = total(2) + 1.0 - cx * (sum_x + far_x)
            m_xy = total(3) + rise_x - cx * sum_y - cy * far_x
            m_yy = total(4) + 7.0 + 2.0 * rise_y - cy * (sum_y + far_y)
            scale = 1.0 / (m_xx * m_yy - m_xy * m_xy)
            i_xx, i_yy, i_xy = m_yy * scale, m_xx * scale, m_xy * scale
            for k in range(3):
                a = af[2 + k, r]
                sum_a, rise_a = column(5 + 3 * k)
                v_x = total(6 + 3 * k) - cx * sum_a - a * far_x
                v_y = total(7 + 3 * k) + rise_a - cy * sum_a - a * far_y
                s_x = i_xx * v_x - i_xy * v_y
                s_y = i_yy * v_y - i_xy * v_x
                pf[k, r + 1] = a - s_x * cx - s_y * cy
                pf[3 + k, r + 1] = s_x
                pf[6 + k, r + 1] = s_y

        each_row(slope_row)
        for k in range(9):
            wrap(pf, k)

        back = LANES - turn

        def push_row(r):
            sums = {}
            off_x, off_y = of[0, r], of[1, r]
            for dx in STEPS:
                to_x = lanes_from(off_x, dx)
                to_x = to_x + dx if dx else to_x
                to_y = lanes_from(off_y, dx)
                total = [None] * 3
                for dy in STEPS:
                    i = r + 1 - dy
                    weight = kb[index_of(dy, dx), i]
                    up = to_y + dy if dy else to_y
                    for k in range(3):
                        value = pf[k, i] + pf[3 + k, i] * to_x + pf[6 + k, i] * up
                        term = weight * value
                        total[k] = term if total[k] is None else total[k] + term
                sums[dx] = [lanes_from(v, -dx) for v in total]
            for k in range(3):
                value = (sums[0][k] + sums[1][k] + sums[-1][k]) * ic[r]
                obuf[k, c, pl.ds(DEPTH + r, SUBS, stride=strip), :] = pltpu.roll(value, back, 1)

        each_row(push_row)

    def tile_step(k, carry):
        c = jnp.where(k < tiles - 1, k + 1, jnp.where(k == tiles - 1, 0, tiles))

        @pl.when(k == tiles - 1)
        def _():
            for group in (2, 0, 1):
                await_all(sideways, group)
            spread_flags(0, tiles - 1, 0)
            spread_flags(2, 0, tiles + 1)

        tile_work(c)
        return carry

    lax.fori_loop(0, tiles + 1, tile_step, 0)

    for t in range(tiles):
        edge = (t + 1) * step - t * LANES + (LANES - 2 * DEPTH - step) // 2
        for r in range(height // SUBS):
            rows = pl.ds(SUBS * (r + 1), SUBS)
            for k in range(3):
                out[k, pl.ds(SUBS * r, SUBS), pl.ds(t * LANES, LANES)] = jnp.where(
                    lane < edge, obuf[k, t, rows, :], obuf[k, t + 1, rows, :]
                )

    for k in range(len(DIRS)):
        @pl.when(exists(*DIRS[k]))
        def _(k=k):
            for group in range(3):
                message(k, group).wait_send()


def body(state, cut_mask, fraction, neighbourhood, tile_flags, centroid_offset):
    height, width = cut_mask.shape
    tiles = width // LANES
    strip = (height + 2 * DEPTH) // SUBS
    step = (width - (LANES - 2 * DEPTH)) // tiles
    assert strip * SUBS == height + 2 * DEPTH and tiles * LANES == width
    assert tile_flags.shape == (1, tiles)
    assert step * tiles + LANES - 2 * DEPTH == width and height % SUBS == 0
    tall = (tiles + 2, height + 2 * SUBS, LANES)
    rows = (strip + 2, SUBS, LANES)
    flat = (strip, SUBS, LANES)
    f32, i32 = jnp.float32, jnp.int32
    return pl.pallas_call(
        kernel,
        out_shape=pltpu.VMEM(state.shape, state.dtype),
        in_specs=[pl.BlockSpec(memory_space=pltpu.HBM)] * 6,
        out_specs=pl.BlockSpec(memory_space=pltpu.VMEM),
        scratch_shapes=[
            pltpu.VMEM((5,) + tall, f32),
            pltpu.VMEM((3,) + tall, i32),
            pltpu.VMEM((3, 3, 1, tiles), i32),
            pltpu.VMEM((3, tiles + 2, SUBS, LANES), i32),
            pltpu.VMEM(flat, i32),
            pltpu.VMEM((3, tiles + 1) + tall[1:], f32),
            pltpu.VMEM(flat, i32),
            pltpu.VMEM(flat, f32),
            pltpu.VMEM((9,) + rows, f32),
            pltpu.VMEM((3,) + rows, f32),
            pltpu.VMEM((2,) + flat, f32),
            pltpu.VMEM(flat, f32),
            pltpu.VMEM((6,) + rows, f32),
            pltpu.VMEM((5,) + flat, f32),
            pltpu.VMEM((14,) + rows, f32),
            pltpu.VMEM((9,) + rows, f32),
            pltpu.SemaphoreType.DMA((5 * tiles + 1,)),
            pltpu.SemaphoreType.DMA((3 * len(DIRS),)),
            pltpu.SemaphoreType.DMA((3 * len(DIRS),)),
        ],
        compiler_params=pltpu.CompilerParams(
            collective_id=0, has_side_effects=True, vmem_limit_bytes=61_500_000
        ),
    )(state, cut_mask, fraction, neighbourhood, tile_flags, centroid_offset)


def solution(mesh):
    placed = (
        P(None, "ty", "tx"),
        P("ty", "tx"),
        P("ty", "tx"),
        P("ty", "tx"),
        P("ty", "tx"),
        P(None, "ty", "tx"),
    )
    return jax.shard_map(
        body, mesh=mesh, in_specs=placed, out_specs=P(None, "ty", "tx"), check_vma=False
    )
```

```python
import functools

import jax
import jax.numpy as jnp
from jax import lax
from jax.experimental import pallas as pl
from jax.experimental.pallas import tpu as pltpu
from jax.sharding import PartitionSpec as P

COURANT = 0.1
LANES = 128
SUBS = 8
DEPTH = 4
TINY = 1.0 / 1024.0
STEPS = (-1, 0, 1)
DIRS = [(dy, dx) for dy in STEPS for dx in STEPS if (dy, dx) != (0, 0)]
GROUPS = (8, 8)


def index_of(dy, dx):
    return 3 * (dy + 1) + dx + 1


def bit_of(dy, dx):
    return 1 << index_of(dy, dx)


def lanes_from(value, step):
    return value if step == 0 else pltpu.roll(value, (-step) % LANES, 1)


def kernel(
    state, mask, fraction, code, flags, offset, out,
    fbuf, ibuf, fl, ft, fr, obuf, ce_, kp_, kb_, st_, of_, ic_, gf_, af_, hf_, pf,
    lsem, ssem, rsem,
):
    ny, nx = lax.axis_size("ty"), lax.axis_size("tx")
    y, x = lax.axis_index("ty"), lax.axis_index("tx")
    height = state.shape[1]
    tiles = state.shape[2] // LANES
    strip = (height + 2 * DEPTH) // SUBS
    inner = pl.ds(SUBS, height)

    def exists(dy, dx):
        good = None
        for step, place, size in ((dy, y, ny), (dx, x, nx)):
            if step:
                here = place > 0 if step < 0 else place < size - 1
                good = here if good is None else good & here
        return good

    barrier = pltpu.get_barrier_semaphore()
    for dy, dx in DIRS:
        @pl.when(exists(dy, dx))
        def _(dy=dy, dx=dx):
            pl.semaphore_signal(
                barrier, inc=1, device_id=(y + dy, x + dx),
                device_id_type=pl.DeviceIdType.MESH,
            )

    local = []
    for t in range(tiles):
        cols = pl.ds(t * LANES, LANES)
        pairs = [
            (mask.at[:, cols], ibuf.at[0, t + 1, inner]),
            (fraction.at[:, cols], ibuf.at[1, t + 1, inner]),
            (code.at[:, cols], ibuf.at[2, t + 1, inner]),
            (state.at[:, :, cols], fbuf.at[pl.ds(0, 3), t + 1, inner]),
            (offset.at[:, :, cols], fbuf.at[pl.ds(3, 2), t + 1, inner]),
        ]
        for src, dst in pairs:
            copy = pltpu.make_async_copy(src, dst, lsem.at[len(local)])
            copy.start()
            local.append(copy)

    copy = pltpu.make_async_copy(flags, fl.at[1, 1], lsem.at[len(local)])
    copy.start()
    local.append(copy)

    rows_of = {-1: pl.ds(DEPTH, DEPTH), 0: inner, 1: pl.ds(SUBS + height, DEPTH)}
    cols_of = {-1: pl.ds(0, 1), 0: pl.ds(1, tiles), 1: pl.ds(tiles + 1, 1)}
    for dy, dx in DIRS:
        @pl.when(jnp.logical_not(exists(dy, dx)))
        def _(dy=dy, dx=dx):
            part = (cols_of[dx], rows_of[dy])
            shape = (cols_of[dx].size, rows_of[dy].size, LANES)
            fl[dy + 1, dx + 1] = jnp.ones((1, tiles), jnp.int32)
            for k in range(5):
                fbuf[(k,) + part] = jnp.zeros(shape, jnp.float32)
            for k in range(3):
                ibuf[(k,) + part] = jnp.full(shape, 1 if k == 0 else 0, jnp.int32)

    for copy in local:
        copy.wait()
    has = lambda good: jnp.where(good, 1, 0).astype(jnp.int32)
    pl.semaphore_wait(barrier, sum(has(exists(dy, dx)) for dy, dx in DIRS))

    def message(k, g):
        dy, dx = DIRS[k]
        where = dict(
            send_sem=ssem.at[3 * k + g],
            recv_sem=rsem.at[3 * k + g],
            device_id=(y + dy, x + dx),
            device_id_type=pl.DeviceIdType.MESH,
        )
        if g == 2:
            return pltpu.make_async_remote_copy(
                src_ref=fl.at[1, 1], dst_ref=fl.at[1 - dy, 1 - dx], **where
            )
        buf = (ibuf, fbuf)[g]
        src_rows = {-1: pl.ds(SUBS, DEPTH), 0: inner, 1: pl.ds(height + DEPTH, DEPTH)}[dy]
        src_cols = {-1: pl.ds(1, 1), 0: pl.ds(1, tiles), 1: pl.ds(tiles, 1)}[dx]
        return pltpu.make_async_remote_copy(
            src_ref=buf.at[:, src_cols, src_rows],
            dst_ref=buf.at[:, cols_of[-dx], rows_of[-dy]],
            **where,
        )

    vertical = [k for k, d in enumerate(DIRS) if d[1] == 0]
    sideways = [k for k, d in enumerate(DIRS) if d[1] != 0]
    corners = [k for k in sideways if DIRS[k][0] != 0]
    level = [k for k in sideways if DIRS[k][0] == 0]
    order = ((2, vertical), (0, vertical), (1, vertical), (2, corners), (0, corners), (1, corners))
    order += ((2, level), (0, level), (1, level))
    for group, ks in order:
        for k in ks:
            @pl.when(exists(*DIRS[k]))
            def _(k=k, group=group):
                message(k, group).start()

    def await_all(ks, group):
        for k in ks:
            dy, dx = DIRS[k]
            @pl.when(exists(-dy, -dx))
            def _(k=k):
                message(k, group).wait_recv()

    def spread_flags(side, tile, place, groups):
        for g in groups:
            value = fl[g, side, :, pl.ds(tile, 1)]
            ft[g, place] = jnp.broadcast_to(value, (SUBS, LANES))

    step = (state.shape[2] - (LANES - 2 * DEPTH)) // tiles
    lane = lax.broadcasted_iota(jnp.int32, (SUBS, LANES), 1)
    sub = lax.broadcasted_iota(jnp.int32, (SUBS, LANES), 0)

    def each_row(fn, rows, size):
        rows = list(rows)
        groups = len(rows) // size if size < len(rows) else 0

        def some(g, carry):
            for k in range(size):
                fn(rows[k] + g * (rows[size] - rows[0]))
            return carry

        if groups:
            lax.fori_loop(0, groups, some, 0)
        for r in rows[groups * size:]:
            fn(r)

    def wrap(ref, *index):
        ref[(*index, 0)] = pltpu.roll(ref[(*index, strip)], 1, 0)
        ref[(*index, strip + 1)] = pltpu.roll(ref[(*index, 1)], SUBS - 1, 0)

    every, early, late = range(3)

    def tile_work(c, phase):
        ce, kp, kb, st, of, ic, gf, af, hf = (
            ref.at[c] for ref in (ce_, kp_, kb_, st_, of_, ic_, gf_, af_, hf_)
        )

        def rows_for(margin):
            low, high = DEPTH + margin, strip - DEPTH - margin
            if phase == every:
                return range(strip)
            if phase == early:
                return range(low, high)
            return [*range(low), *range(high, strip)]

        turn = DEPTH + c * (LANES - step)
        first = lane >= LANES - turn

        def flags_of(g):
            return jnp.where(first, ft[g, c], ft[g, c + 1])

        flag = [None if phase == early and g != 1 else flags_of(g) for g in range(3)]
        for r in rows_for(0):
            value = flag[1]
            if r < DEPTH:
                value = jnp.where(sub == 0, flag[0], value)
            if r >= strip - DEPTH:
                value = jnp.where(sub == SUBS - 1, flag[2], value)
            fr[r] = value

        def load_row(r):
            rows = pl.ds(DEPTH + r, SUBS, stride=strip)

            def pick(buf, k):
                return jnp.where(first, buf[k, c, rows, :], buf[k, c + 1, rows, :])

            def turned(value):
                return pltpu.roll(value, turn, 1)

            on = pick(ibuf, 0) * fr[r] > 0
            bits = turned(jnp.where(on, pick(ibuf, 2), 16))
            kappa = turned(
                jnp.where(on, pick(ibuf, 1).astype(jnp.float32) * (1.0 / 1024.0), 1.0)
            )
            ce[r] = bits
            kp[r] = kappa
            for b in range(9):
                kb[b, r + 1] = jnp.where((bits & (1 << b)) != 0, kappa, 0.0)
            for k in range(3):
                st[k, r + 1] = turned(pick(fbuf, k))
            for k in range(2):
                of[k, r] = turned(jnp.where(on, pick(fbuf, 3 + k), 0.0))

        each_row(load_row, rows_for(0), strip)
        if phase != early:
            for k in range(9):
                wrap(kb, k)
            for k in range(3):
                wrap(st, k)

        def share_row(r):
            sums = {}
            for dx in STEPS:
                parts = [kb[index_of(dy, dx), r + 1 - dy] for dy in STEPS]
                sums[dx] = parts[0] + parts[1] + parts[2]
            cover = sums[0] + lanes_from(sums[1], -1) + lanes_from(sums[-1], 1)
            inv_cover = 1.0 / jnp.maximum(cover, TINY)
            ic[r] = inv_cover
            kappa = kp[r]
            share = kappa * inv_cover
            rate = (0.5 * COURANT) / jnp.maximum(kappa, TINY)
            here = [st[k, r + 1] for k in range(3)]
            east = [lanes_from(v, 1) for v in here]
            west = [lanes_from(v, -1) for v in here]
            north = [st[k, r + 2] for k in range(3)]
            south = [st[k, r] for k in range(3)]
            flux = [
                (east[1] - west[1]) + (north[2] - south[2]),
                east[0] - west[0],
                north[0] - south[0],
            ]
            gf[0, r + 1] = share
            gf[1, r + 1] = share * of[0, r]
            gf[2, r + 1] = share * of[1, r]
            for k in range(3):
                smooth = (east[k] + west[k]) + (north[k] + south[k]) - 4.0 * here[k]
                gf[3 + k, r + 1] = share * (here[k] - rate * (flux[k] - smooth))

        each_row(share_row, rows_for(1), strip)
        if phase != early:
            for k in range(6):
                wrap(gf, k)

        def gather_row(r):
            own = ce[r]
            rows = {dy: [gf[k, r + 1 + dy] for k in range(6)] for dy in STEPS}
            for dy in (-1, 1):
                rows[dy][2] = rows[dy][2] + dy * rows[dy][0]
            sums = {}
            for dx in STEPS:
                moved = lanes_from(own, -dx)
                total = [None] * 6
                for dy in STEPS:
                    member = (moved & bit_of(dy, dx)) != 0
                    for k in range(6):
                        term = jnp.where(member, rows[dy][k], 0.0)
                        total[k] = term if total[k] is None else total[k] + term
                sums[dx] = [lanes_from(v, dx) for v in total]
            whole = [sums[0][k] + sums[1][k] + sums[-1][k] for k in range(6)]
            inv_total = 1.0 / jnp.maximum(whole[0], TINY)
            cx = (whole[1] + (sums[1][0] - sums[-1][0])) * inv_total
            cy = whole[2] * inv_total
            av = [whole[3 + k] * inv_total for k in range(3)]
            ux = [lanes_from(cx, -1) - 1.0, cx, lanes_from(cx, 1) + 1.0]
            uy = [lanes_from(cy, dx) for dx in STEPS]

            def dot(left, right):
                return left[0] * right[0] + left[1] * right[1] + left[2] * right[2]

            values = [ux[0] + ux[1] + ux[2], uy[0] + uy[1] + uy[2]]
            values += [dot(ux, ux), dot(ux, uy), dot(uy, uy)]
            for k in range(3):
                near = [lanes_from(av[k], dx) for dx in STEPS]
                values += [near[0] + near[1] + near[2], dot(ux, near), dot(uy, near)]
            for k, v in enumerate(values):
                hf[k, r + 1] = v
            for k, v in enumerate([cx, cy] + av):
                af[k, r] = v

        each_row(gather_row, rows_for(2), DEPTH + 2 if phase == late else 8)
        if phase == early:
            return
        for k in range(14):
            wrap(hf, k)

        def slope_row(r):
            def column(k):
                low, high = hf[k, r], hf[k, r + 2]
                return low + hf[k, r + 1] + high, high - low

            def total(k):
                return hf[k, r] + hf[k, r + 1] + hf[k, r + 2]

            cx, cy = af[0, r], af[1, r]
            sum_x, rise_x = column(0)
            sum_y, rise_y = column(1)
            far_x, far_y = sum_x - 9.0 * cx, sum_y - 9.0 * cy
            m_xx = total(2) + 1.0 - cx * (sum_x + far_x)
            m_xy = total(3) + rise_x - cx * sum_y - cy * far_x
            m_yy = total(4) + 7.0 + 2.0 * rise_y - cy * (sum_y + far_y)
            scale = 1.0 / (m_xx * m_yy - m_xy * m_xy)
            i_xx, i_yy, i_xy = m_yy * scale, m_xx * scale, m_xy * scale
            for k in range(3):
                a = af[2 + k, r]
                sum_a, rise_a = column(5 + 3 * k)
                v_x = total(6 + 3 * k) - cx * sum_a - a * far_x
                v_y = total(7 + 3 * k) + rise_a - cy * sum_a - a * far_y
                s_x = i_xx * v_x - i_xy * v_y
                s_y = i_yy * v_y - i_xy * v_x
                pf[k, r + 1] = a - s_x * cx - s_y * cy
                pf[3 + k, r + 1] = s_x
                pf[6 + k, r + 1] = s_y

        each_row(slope_row, range(strip), GROUPS[0])
        for k in range(9):
            wrap(pf, k)

        back = LANES - turn

        def push_row(r):
            sums = {}
            off_x, off_y = of[0, r], of[1, r]
            for dx in STEPS:
                to_x = lanes_from(off_x, dx)
                to_x = to_x + dx if dx else to_x
                to_y = lanes_from(off_y, dx)
                total = [None] * 3
                for dy in STEPS:
                    i = r + 1 - dy
                    weight = kb[index_of(dy, dx), i]
                    up = to_y + dy if dy else to_y
                    for k in range(3):
                        value = pf[k, i] + pf[3 + k, i] * to_x + pf[6 + k, i] * up
                        term = weight * value
                        total[k] = term if total[k] is None else total[k] + term
                sums[dx] = [lanes_from(v, -dx) for v in total]
            for k in range(3):
                value = (sums[0][k] + sums[1][k] + sums[-1][k]) * ic[r]
                obuf[k, c, pl.ds(DEPTH + r, SUBS, stride=strip), :] = pltpu.roll(value, back, 1)

        each_row(push_row, range(strip), GROUPS[1])

    def inner_early(c, carry):
        tile_work(c, early)
        return carry

    def inner_late(c, carry):
        tile_work(c, late)
        return carry

    def outer(k, carry):
        tile_work(k * tiles, every)
        return carry

    for t in range(tiles):
        spread_flags(1, t, t + 1, (1,))
    lax.fori_loop(1, tiles, inner_early, 0)
    for group in (2, 0, 1):
        await_all(vertical, group)
    for t in range(tiles):
        spread_flags(1, t, t + 1, (0, 2))
    lax.fori_loop(1, tiles, inner_late, 0)
    for group in (2, 0, 1):
        await_all(sideways, group)
    spread_flags(0, tiles - 1, 0, range(3))
    spread_flags(2, 0, tiles + 1, range(3))
    lax.fori_loop(0, 2, outer, 0)

    for t in range(tiles):
        edge = (t + 1) * step - t * LANES + (LANES - 2 * DEPTH - step) // 2
        for r in range(height // SUBS):
            rows = pl.ds(SUBS * (r + 1), SUBS)
            for k in range(3):
                out[k, pl.ds(SUBS * r, SUBS), pl.ds(t * LANES, LANES)] = jnp.where(
                    lane < edge, obuf[k, t, rows, :], obuf[k, t + 1, rows, :]
                )

    for k in range(len(DIRS)):
        @pl.when(exists(*DIRS[k]))
        def _(k=k):
            for group in range(3):
                message(k, group).wait_send()


def body(state, cut_mask, fraction, neighbourhood, tile_flags, centroid_offset):
    height, width = cut_mask.shape
    tiles = width // LANES
    strip = (height + 2 * DEPTH) // SUBS
    step = (width - (LANES - 2 * DEPTH)) // tiles
    assert strip * SUBS == height + 2 * DEPTH and tiles * LANES == width
    assert tile_flags.shape == (1, tiles)
    assert step * tiles + LANES - 2 * DEPTH == width and height % SUBS == 0
    tall = (tiles + 2, height + 2 * SUBS, LANES)
    rows = (strip + 2, SUBS, LANES)
    flat = (strip, SUBS, LANES)
    each = (tiles + 1,)
    f32, i32 = jnp.float32, jnp.int32
    return pl.pallas_call(
        kernel,
        out_shape=pltpu.VMEM(state.shape, state.dtype),
        in_specs=[pl.BlockSpec(memory_space=pltpu.HBM)] * 6,
        out_specs=pl.BlockSpec(memory_space=pltpu.VMEM),
        scratch_shapes=[
            pltpu.VMEM((5,) + tall, f32),
            pltpu.VMEM((3,) + tall, i32),
            pltpu.VMEM((3, 3, 1, tiles), i32),
            pltpu.VMEM((3, tiles + 2, SUBS, LANES), i32),
            pltpu.VMEM(flat, i32),
            pltpu.VMEM((3, tiles + 1) + tall[1:], f32),
            pltpu.VMEM(each + flat, i32),
            pltpu.VMEM(each + flat, f32),
            pltpu.VMEM(each + (9,) + rows, f32),
            pltpu.VMEM(each + (3,) + rows, f32),
            pltpu.VMEM(each + (2,) + flat, f32),
            pltpu.VMEM(each + flat, f32),
            pltpu.VMEM(each + (6,) + rows, f32),
            pltpu.VMEM(each + (5,) + flat, f32),
            pltpu.VMEM(each + (14,) + rows, f32),
            pltpu.VMEM((9,) + rows, f32),
            pltpu.SemaphoreType.DMA((5 * tiles + 1,)),
            pltpu.SemaphoreType.DMA((3 * len(DIRS),)),
            pltpu.SemaphoreType.DMA((3 * len(DIRS),)),
        ],
        compiler_params=pltpu.CompilerParams(
            collective_id=0, has_side_effects=True, vmem_limit_bytes=61_500_000
        ),
    )(state, cut_mask, fraction, neighbourhood, tile_flags, centroid_offset)


def solution(mesh):
    placed = (
        P(None, "ty", "tx"),
        P("ty", "tx"),
        P("ty", "tx"),
        P("ty", "tx"),
        P("ty", "tx"),
        P(None, "ty", "tx"),
    )
    return jax.shard_map(
        body, mesh=mesh, in_specs=placed, out_specs=P(None, "ty", "tx"), check_vma=False
    )
```

```python
import functools

import jax
import jax.numpy as jnp
from jax import lax
from jax.experimental import pallas as pl
from jax.experimental.pallas import tpu as pltpu
from jax.sharding import PartitionSpec as P

COURANT = 0.1
LANES = 128
SUBS = 8
DEPTH = 4
TINY = 1.0 / 1024.0
STEPS = (-1, 0, 1)
DIRS = [(dy, dx) for dy in STEPS for dx in STEPS if (dy, dx) != (0, 0)]
GROUPS = (8, 8)


def index_of(dy, dx):
    return 3 * (dy + 1) + dx + 1


def bit_of(dy, dx):
    return 1 << index_of(dy, dx)


def lanes_from(value, step):
    return value if step == 0 else pltpu.roll(value, (-step) % LANES, 1)


def kernel(
    state, mask, fraction, code, flags, offset, out,
    fbuf, ibuf, fl, ft, fr, obuf, ce_, kp_, kb_, st_, of_, ic_, gf_, af_, hf_, pf_,
    lsem, ssem, rsem,
):
    ny, nx = lax.axis_size("ty"), lax.axis_size("tx")
    y, x = lax.axis_index("ty"), lax.axis_index("tx")
    height = state.shape[1]
    tiles = state.shape[2] // LANES
    strip = (height + 2 * DEPTH) // SUBS
    inner = pl.ds(SUBS, height)

    def exists(dy, dx):
        good = None
        for step, place, size in ((dy, y, ny), (dx, x, nx)):
            if step:
                here = place > 0 if step < 0 else place < size - 1
                good = here if good is None else good & here
        return good

    barrier = pltpu.get_barrier_semaphore()
    for dy, dx in DIRS:
        @pl.when(exists(dy, dx))
        def _(dy=dy, dx=dx):
            pl.semaphore_signal(
                barrier, inc=1, device_id=(y + dy, x + dx),
                device_id_type=pl.DeviceIdType.MESH,
            )

    local = []
    for t in range(tiles):
        cols = pl.ds(t * LANES, LANES)
        pairs = [
            (mask.at[:, cols], ibuf.at[0, t + 1, inner]),
            (fraction.at[:, cols], ibuf.at[1, t + 1, inner]),
            (code.at[:, cols], ibuf.at[2, t + 1, inner]),
            (state.at[:, :, cols], fbuf.at[pl.ds(0, 3), t + 1, inner]),
            (offset.at[:, :, cols], fbuf.at[pl.ds(3, 2), t + 1, inner]),
        ]
        for src, dst in pairs:
            copy = pltpu.make_async_copy(src, dst, lsem.at[len(local)])
            copy.start()
            local.append(copy)

    copy = pltpu.make_async_copy(flags, fl.at[1, 1], lsem.at[len(local)])
    copy.start()
    local.append(copy)

    rows_of = {-1: pl.ds(DEPTH, DEPTH), 0: inner, 1: pl.ds(SUBS + height, DEPTH)}
    cols_of = {-1: pl.ds(0, 1), 0: pl.ds(1, tiles), 1: pl.ds(tiles + 1, 1)}
    for dy, dx in DIRS:
        @pl.when(jnp.logical_not(exists(dy, dx)))
        def _(dy=dy, dx=dx):
            part = (cols_of[dx], rows_of[dy])
            shape = (cols_of[dx].size, rows_of[dy].size, LANES)
            fl[dy + 1, dx + 1] = jnp.ones((1, tiles), jnp.int32)
            for k in range(5):
                fbuf[(k,) + part] = jnp.zeros(shape, jnp.float32)
            for k in range(3):
                ibuf[(k,) + part] = jnp.full(shape, 1 if k == 0 else 0, jnp.int32)

    for copy in local:
        copy.wait()
    has = lambda good: jnp.where(good, 1, 0).astype(jnp.int32)
    pl.semaphore_wait(barrier, sum(has(exists(dy, dx)) for dy, dx in DIRS))

    def message(k, g):
        dy, dx = DIRS[k]
        where = dict(
            send_sem=ssem.at[3 * k + g],
            recv_sem=rsem.at[3 * k + g],
            device_id=(y + dy, x + dx),
            device_id_type=pl.DeviceIdType.MESH,
        )
        if g == 2:
            return pltpu.make_async_remote_copy(
                src_ref=fl.at[1, 1], dst_ref=fl.at[1 - dy, 1 - dx], **where
            )
        buf = (ibuf, fbuf)[g]
        src_rows = {-1: pl.ds(SUBS, DEPTH), 0: inner, 1: pl.ds(height + DEPTH, DEPTH)}[dy]
        src_cols = {-1: pl.ds(1, 1), 0: pl.ds(1, tiles), 1: pl.ds(tiles, 1)}[dx]
        return pltpu.make_async_remote_copy(
            src_ref=buf.at[:, src_cols, src_rows],
            dst_ref=buf.at[:, cols_of[-dx], rows_of[-dy]],
            **where,
        )

    vertical = [k for k, d in enumerate(DIRS) if d[1] == 0]
    sideways = [k for k, d in enumerate(DIRS) if d[1] != 0]
    corners = [k for k in sideways if DIRS[k][0] != 0]
    level = [k for k in sideways if DIRS[k][0] == 0]
    order = ((2, vertical), (0, vertical), (1, vertical), (2, corners), (0, corners), (1, corners))
    order += ((2, level), (0, level), (1, level))
    for group, ks in order:
        for k in ks:
            @pl.when(exists(*DIRS[k]))
            def _(k=k, group=group):
                message(k, group).start()

    def await_all(ks, group):
        for k in ks:
            dy, dx = DIRS[k]
            @pl.when(exists(-dy, -dx))
            def _(k=k):
                message(k, group).wait_recv()

    def spread_flags(side, tile, place, groups):
        for g in groups:
            value = fl[g, side, :, pl.ds(tile, 1)]
            ft[g, place] = jnp.broadcast_to(value, (SUBS, LANES))

    step = (state.shape[2] - (LANES - 2 * DEPTH)) // tiles
    lane = lax.broadcasted_iota(jnp.int32, (SUBS, LANES), 1)
    sub = lax.broadcasted_iota(jnp.int32, (SUBS, LANES), 0)

    def each_row(fn, rows, size):
        rows = list(rows)
        groups = len(rows) // size if size < len(rows) else 0

        def some(g, carry):
            for k in range(size):
                fn(rows[k] + g * (rows[size] - rows[0]))
            return carry

        if groups:
            lax.fori_loop(0, groups, some, 0)
        for r in rows[groups * size:]:
            fn(r)

    def wrap(ref, *index):
        ref[(*index, 0)] = pltpu.roll(ref[(*index, strip)], 1, 0)
        ref[(*index, strip + 1)] = pltpu.roll(ref[(*index, 1)], SUBS - 1, 0)

    every, early, late = range(3)

    def tile_work(c, phase):
        ce, kp, kb, st, of, ic, gf, af, hf, pf = (
            ref.at[c] for ref in (ce_, kp_, kb_, st_, of_, ic_, gf_, af_, hf_, pf_)
        )

        def rows_for(margin):
            low, high = DEPTH + margin, strip - DEPTH - margin
            if phase == every:
                return range(strip)
            if phase == early:
                return range(low, high)
            return [*range(low), *range(high, strip)]

        turn = DEPTH + c * (LANES - step)
        first = lane >= LANES - turn

        def flags_of(g):
            return jnp.where(first, ft[g, c], ft[g, c + 1])

        flag = [None if phase == early and g != 1 else flags_of(g) for g in range(3)]
        for r in rows_for(0):
            value = flag[1]
            if r < DEPTH:
                value = jnp.where(sub == 0, flag[0], value)
            if r >= strip - DEPTH:
                value = jnp.where(sub == SUBS - 1, flag[2], value)
            fr[r] = value

        def load_row(r):
            rows = pl.ds(DEPTH + r, SUBS, stride=strip)

            def pick(buf, k):
                return jnp.where(first, buf[k, c, rows, :], buf[k, c + 1, rows, :])

            def turned(value):
                return pltpu.roll(value, turn, 1)

            on = pick(ibuf, 0) * fr[r] > 0
            bits = turned(jnp.where(on, pick(ibuf, 2), 16))
            kappa = turned(
                jnp.where(on, pick(ibuf, 1).astype(jnp.float32) * (1.0 / 1024.0), 1.0)
            )
            ce[r] = bits
            kp[r] = kappa
            for b in range(9):
                kb[b, r + 1] = jnp.where((bits & (1 << b)) != 0, kappa, 0.0)
            for k in range(3):
                st[k, r + 1] = turned(pick(fbuf, k))
            for k in range(2):
                of[k, r] = turned(jnp.where(on, pick(fbuf, 3 + k), 0.0))

        each_row(load_row, rows_for(0), strip)
        if phase != early:
            for k in range(9):
                wrap(kb, k)
            for k in range(3):
                wrap(st, k)

        def share_row(r):
            sums = {}
            for dx in STEPS:
                parts = [kb[index_of(dy, dx), r + 1 - dy] for dy in STEPS]
                sums[dx] = parts[0] + parts[1] + parts[2]
            cover = sums[0] + lanes_from(sums[1], -1) + lanes_from(sums[-1], 1)
            inv_cover = 1.0 / jnp.maximum(cover, TINY)
            ic[r] = inv_cover
            kappa = kp[r]
            share = kappa * inv_cover
            rate = (0.5 * COURANT) / jnp.maximum(kappa, TINY)
            here = [st[k, r + 1] for k in range(3)]
            east = [lanes_from(v, 1) for v in here]
            west = [lanes_from(v, -1) for v in here]
            north = [st[k, r + 2] for k in range(3)]
            south = [st[k, r] for k in range(3)]
            flux = [
                (east[1] - west[1]) + (north[2] - south[2]),
                east[0] - west[0],
                north[0] - south[0],
            ]
            gf[0, r + 1] = share
            gf[1, r + 1] = share * of[0, r]
            gf[2, r + 1] = share * of[1, r]
            for k in range(3):
                smooth = (east[k] + west[k]) + (north[k] + south[k]) - 4.0 * here[k]
                gf[3 + k, r + 1] = share * (here[k] - rate * (flux[k] - smooth))

        each_row(share_row, rows_for(1), strip)
        if phase != early:
            for k in range(6):
                wrap(gf, k)

        def gather_row(r):
            own = ce[r]
            rows = {dy: [gf[k, r + 1 + dy] for k in range(6)] for dy in STEPS}
            for dy in (-1, 1):
                rows[dy][2] = rows[dy][2] + dy * rows[dy][0]
            sums = {}
            for dx in STEPS:
                moved = lanes_from(own, -dx)
                total = [None] * 6
                for dy in STEPS:
                    member = (moved & bit_of(dy, dx)) != 0
                    for k in range(6):
                        term = jnp.where(member, rows[dy][k], 0.0)
                        total[k] = term if total[k] is None else total[k] + term
                sums[dx] = [lanes_from(v, dx) for v in total]
            whole = [sums[0][k] + sums[1][k] + sums[-1][k] for k in range(6)]
            inv_total = 1.0 / jnp.maximum(whole[0], TINY)
            cx = (whole[1] + (sums[1][0] - sums[-1][0])) * inv_total
            cy = whole[2] * inv_total
            av = [whole[3 + k] * inv_total for k in range(3)]
            ux = [lanes_from(cx, -1) - 1.0, cx, lanes_from(cx, 1) + 1.0]
            uy = [lanes_from(cy, dx) for dx in STEPS]

            def dot(left, right):
                return left[0] * right[0] + left[1] * right[1] + left[2] * right[2]

            values = [ux[0] + ux[1] + ux[2], uy[0] + uy[1] + uy[2]]
            values += [dot(ux, ux), dot(ux, uy), dot(uy, uy)]
            for k in range(3):
                near = [lanes_from(av[k], dx) for dx in STEPS]
                values += [near[0] + near[1] + near[2], dot(ux, near), dot(uy, near)]
            for k, v in enumerate(values):
                hf[k, r + 1] = v
            for k, v in enumerate([cx, cy] + av):
                af[k, r] = v

        each_row(gather_row, rows_for(2), DEPTH + 2 if phase == late else 8)
        if phase != early:
            for k in range(14):
                wrap(hf, k)

        def slope_row(r):
            def column(k):
                low, high = hf[k, r], hf[k, r + 2]
                return low + hf[k, r + 1] + high, high - low

            def total(k):
                return hf[k, r] + hf[k, r + 1] + hf[k, r + 2]

            cx, cy = af[0, r], af[1, r]
            sum_x, rise_x = column(0)
            sum_y, rise_y = column(1)
            far_x, far_y = sum_x - 9.0 * cx, sum_y - 9.0 * cy
            m_xx = total(2) + 1.0 - cx * (sum_x + far_x)
            m_xy = total(3) + rise_x - cx * sum_y - cy * far_x
            m_yy = total(4) + 7.0 + 2.0 * rise_y - cy * (sum_y + far_y)
            scale = 1.0 / (m_xx * m_yy - m_xy * m_xy)
            i_xx, i_yy, i_xy = m_yy * scale, m_xx * scale, m_xy * scale
            for k in range(3):
                a = af[2 + k, r]
                sum_a, rise_a = column(5 + 3 * k)
                v_x = total(6 + 3 * k) - cx * sum_a - a * far_x
                v_y = total(7 + 3 * k) + rise_a - cy * sum_a - a * far_y
                s_x = i_xx * v_x - i_xy * v_y
                s_y = i_yy * v_y - i_xy * v_x
                pf[k, r + 1] = a - s_x * cx - s_y * cy
                pf[3 + k, r + 1] = s_x
                pf[6 + k, r + 1] = s_y

        each_row(slope_row, rows_for(3), DEPTH + 3 if phase == late else GROUPS[0])
        if phase != early:
            for k in range(9):
                wrap(pf, k)

        back = LANES - turn

        def push_row(r):
            sums = {}
            off_x, off_y = of[0, r], of[1, r]
            for dx in STEPS:
                to_x = lanes_from(off_x, dx)
                to_x = to_x + dx if dx else to_x
                to_y = lanes_from(off_y, dx)
                total = [None] * 3
                for dy in STEPS:
                    i = r + 1 - dy
                    weight = kb[index_of(dy, dx), i]
                    up = to_y + dy if dy else to_y
                    for k in range(3):
                        value = pf[k, i] + pf[3 + k, i] * to_x + pf[6 + k, i] * up
                        term = weight * value
                        total[k] = term if total[k] is None else total[k] + term
                sums[dx] = [lanes_from(v, -dx) for v in total]
            for k in range(3):
                value = (sums[0][k] + sums[1][k] + sums[-1][k]) * ic[r]
                obuf[k, c, pl.ds(DEPTH + r, SUBS, stride=strip), :] = pltpu.roll(value, back, 1)

        each_row(push_row, rows_for(4), DEPTH + 4 if phase == late else GROUPS[1])

    def inner_early(c, carry):
        tile_work(c, early)
        return carry

    def inner_late(c, carry):
        tile_work(c, late)
        return carry

    def outer(k, carry):
        tile_work(k * tiles, every)
        return carry

    for t in range(tiles):
        spread_flags(1, t, t + 1, (1,))
    lax.fori_loop(1, tiles, inner_early, 0)
    for group in (2, 0, 1):
        await_all(vertical, group)
    for t in range(tiles):
        spread_flags(1, t, t + 1, (0, 2))
    lax.fori_loop(1, tiles, inner_late, 0)
    for group in (2, 0, 1):
        await_all(sideways, group)
    spread_flags(0, tiles - 1, 0, range(3))
    spread_flags(2, 0, tiles + 1, range(3))
    lax.fori_loop(0, 2, outer, 0)

    for t in range(tiles):
        edge = (t + 1) * step - t * LANES + (LANES - 2 * DEPTH - step) // 2
        for r in range(height // SUBS):
            rows = pl.ds(SUBS * (r + 1), SUBS)
            for k in range(3):
                out[k, pl.ds(SUBS * r, SUBS), pl.ds(t * LANES, LANES)] = jnp.where(
                    lane < edge, obuf[k, t, rows, :], obuf[k, t + 1, rows, :]
                )

    for k in range(len(DIRS)):
        @pl.when(exists(*DIRS[k]))
        def _(k=k):
            for group in range(3):
                message(k, group).wait_send()


def body(state, cut_mask, fraction, neighbourhood, tile_flags, centroid_offset):
    height, width = cut_mask.shape
    tiles = width // LANES
    strip = (height + 2 * DEPTH) // SUBS
    step = (width - (LANES - 2 * DEPTH)) // tiles
    assert strip * SUBS == height + 2 * DEPTH and tiles * LANES == width
    assert tile_flags.shape == (1, tiles)
    assert step * tiles + LANES - 2 * DEPTH == width and height % SUBS == 0
    tall = (tiles + 2, height + 2 * SUBS, LANES)
    rows = (strip + 2, SUBS, LANES)
    flat = (strip, SUBS, LANES)
    each = (tiles + 1,)
    f32, i32 = jnp.float32, jnp.int32
    return pl.pallas_call(
        kernel,
        out_shape=pltpu.VMEM(state.shape, state.dtype),
        in_specs=[pl.BlockSpec(memory_space=pltpu.HBM)] * 6,
        out_specs=pl.BlockSpec(memory_space=pltpu.VMEM),
        scratch_shapes=[
            pltpu.VMEM((5,) + tall, f32),
            pltpu.VMEM((3,) + tall, i32),
            pltpu.VMEM((3, 3, 1, tiles), i32),
            pltpu.VMEM((3, tiles + 2, SUBS, LANES), i32),
            pltpu.VMEM(flat, i32),
            pltpu.VMEM((3, tiles + 1) + tall[1:], f32),
            pltpu.VMEM(each + flat, i32),
            pltpu.VMEM(each + flat, f32),
            pltpu.VMEM(each + (9,) + rows, f32),
            pltpu.VMEM(each + (3,) + rows, f32),
            pltpu.VMEM(each + (2,) + flat, f32),
            pltpu.VMEM(each + flat, f32),
            pltpu.VMEM(each + (6,) + rows, f32),
            pltpu.VMEM(each + (5,) + flat, f32),
            pltpu.VMEM(each + (14,) + rows, f32),
            pltpu.VMEM(each + (9,) + rows, f32),
            pltpu.SemaphoreType.DMA((5 * tiles + 1,)),
            pltpu.SemaphoreType.DMA((3 * len(DIRS),)),
            pltpu.SemaphoreType.DMA((3 * len(DIRS),)),
        ],
        compiler_params=pltpu.CompilerParams(
            collective_id=0, has_side_effects=True, vmem_limit_bytes=61_500_000
        ),
    )(state, cut_mask, fraction, neighbourhood, tile_flags, centroid_offset)


def solution(mesh):
    placed = (
        P(None, "ty", "tx"),
        P("ty", "tx"),
        P("ty", "tx"),
        P("ty", "tx"),
        P("ty", "tx"),
        P(None, "ty", "tx"),
    )
    return jax.shard_map(
        body, mesh=mesh, in_specs=placed, out_specs=P(None, "ty", "tx"), check_vma=False
    )
```
